256 devices in a mesh: ep: 64 (over z, y, core), tp: 4 (over x).
Axes of the slice: x: 4, y: 4, z: 8, core: 2. Of those that a mesh axis runs over, the one named last changes fastest.
Arguments:
- tokens: bfloat16 [8192, 4096], P('ep', 'tp'), may hold values from -6 to 6
- out_grad: bfloat16 [8192, 4096], P('ep', 'tp'), may hold values from -6 to 6
- expert_ids: int32 [8192, 8], P('ep'), may hold values from 0 to 63, all different within a row; in each aligned block of 128 rows (0 to 127, 128 to 255, ...) at most 18 rows name the same one
- route_probs: float32 [8192, 8], P('ep'), may hold values from 0.05 to 0.5
- w_gate: bfloat16 [64, 4096, 768], P('ep', 'tp'), may hold values from -0.09375 to 0.09375
- w_up: bfloat16 [64, 4096, 768], P('ep', 'tp'), may hold values from -0.09375 to 0.09375
- w_down: bfloat16 [64, 768, 4096], P('ep', None, 'tp'), may hold values from -0.21875 to 0.21875
Outputs:
- grad_tokens: bfloat16 [8192, 4096], P('ep', 'tp')
- fisher_gate: bfloat16 [64, 4096, 768], P('ep', 'tp')
- fisher_up: bfloat16 [64, 4096, 768], P('ep', 'tp')
- fisher_down: bfloat16 [64, 768, 4096], P('ep', None, 'tp')
The draws below stay inside these ranges and needn't reach their ends.
Inputs may be any that keep to these rules, and one draw needn't show every extreme that they name: `expert_ids`: each token names 8 different experts; among the tokens of one index of ep no expert is named by more than 18 tokens, a bound that some block reaches.
All inputs are finite; a program needn't handle non-finite values.
Results may differ from the reference program's by a relative error of at most 0.03.
Values may be sent and summed in bfloat16 or wider, within the bound.
No kernel may reach another device: no remote copies, remote signals or barrier semaphores. Data moves between devices by JAX's collectives and lax.ppermute only.
A program may use at most 128 MiB of HBM per device.

```python
import math
import jax
import jax.numpy as jnp
import numpy as np
from jax import lax

D = 4096
FF = 768
TOK_DEV = 128
TOKENS = 8192
EXPERTS = 64
TOPK = 8
CAP = 18
N_EP = 64
N_TP = 4


def block_levels(stream_key, extent, shards, low, high):
    loudness, own = 1.0, jax.random.fold_in(stream_key, 6)
    for axis_at, blocks in shards:
        draws = jnp.exp(jax.random.uniform(jax.random.fold_in(own, axis_at), (blocks,), jnp.float32, low / len(shards), high / len(shards)))
        loudness = loudness * jnp.repeat(draws, extent[axis_at] // blocks).reshape([-1 if axis == axis_at else 1 for axis in range(len(extent))])
    return loudness


def routed_block(rng, own, number, rows, count, top, bound, skew):
    order = jax.random.permutation(rng, count)
    packed, common = load_shares(count, rows * top, bound, skew, True), load_shares(count, rows * top, bound, skew, False)
    places = jnp.arange(count)

    def named(lengths, rotation):
        used = int((lengths > 0).sum())
        fixed = max(1, used // 4)
        moved = fixed + (places - fixed + rotation * (used - fixed)) % max(1, count - fixed)
        return jnp.zeros((count,), jnp.int32).at[order[jnp.where(places < fixed, places, moved)]].set(jnp.asarray(lengths, jnp.int32))

    lengths = jnp.where(number % 4 == 0, named(packed, number // 4), named(common, number - number // 4 - 1))
    mixed = jax.random.permutation(jax.random.fold_in(own, 3), count)
    giver, sink = mixed[0:count // 2 * 2:2], mixed[1:count // 2 * 2:2]
    room = jnp.minimum(lengths[giver] - 1, bound - lengths[sink]) // 2
    room = jnp.where((giver == order[0]) | (sink == order[0]) | (lengths[sink] == 0), 0, jnp.maximum(room, 0))
    moved = jax.random.randint(jax.random.fold_in(own, 4), (count // 2,), 0, 1 << 20) % (room + 1)
    lengths = lengths.at[giver].add(-moved).at[sink].add(moved)
    labels = jnp.searchsorted(jnp.cumsum(lengths), jnp.arange(rows * top), side="right").astype(jnp.int32)
    grid = labels.reshape(top, rows).T
    grid = grid[jax.random.permutation(jax.random.fold_in(own, 1), rows)]
    rotation = jax.random.randint(jax.random.fold_in(own, 2), (rows, 1), 0, top)
    return jnp.take_along_axis(grid, (jnp.arange(top)[None, :] + rotation) % top, axis=1)


def load_shares(number_of, total, reach, slope, full):
    loads = [(1 << 20) // math.isqrt(standing ** slope) + 1 for standing in range(1, number_of + 1)]
    largest = reach if full else min(reach, max(-(-total // number_of), total * loads[0] // sum(loads)))
    least = 1 if total - largest >= number_of - 1 else 0
    given, surplus = [largest] + [least] * (number_of - 1), total - largest - least * (number_of - 1)
    while surplus > 0:
        free = [i for i in range(1, number_of) if given[i] < largest] or [i for i in range(1, number_of) if given[i] < reach]
        whole, left = sum([loads[i] for i in free]), surplus
        for i in free:
            more = min(reach - given[i], max(1, left * loads[i] // whole), surplus)
            given[i] = given[i] + more
            surplus = surplus - more
    return np.array(given)


def normal_values(key, extent, scale, bound, cuts=(), held_as=jnp.bfloat16):
    values = jax.random.normal(key, extent, jnp.float32) * scale
    if len(cuts) > 0:
        values = block_levels(key, extent, cuts, -0.22, 0.18) * values
    return jnp.clip(values, min=-bound, max=bound).astype(held_as)


def setup_inputs(seed: int = 0) -> dict:
    key_list = jax.random.split(jax.random.key(seed), 8)
    tokens = normal_values(key_list[0], (TOKENS, D), 1.0, 6.0, ((0, 64), (1, 4)))
    out_grad = normal_values(key_list[1], (TOKENS, D), 1.0, 6.0, ((0, 64), (1, 4)))
    expert_ids_keys = jax.random.split(jax.random.fold_in(key_list[2], 1), TOKENS // TOK_DEV)
    expert_ids_turns = jax.random.permutation(jax.random.fold_in(key_list[2], 3), TOKENS // TOK_DEV)
    expert_ids = jax.vmap(lambda own, number: routed_block(jax.random.fold_in(key_list[2], 2), own, number, TOK_DEV, EXPERTS, TOPK, CAP, 2))(expert_ids_keys, expert_ids_turns).reshape((TOKENS, TOPK))
    route_probs = jnp.clip(jnp.exp(math.log(0.5) - 2.3025851 * jax.random.uniform(key_list[3], (TOKENS, TOPK), jnp.float32) ** block_levels(key_list[3], (TOKENS, TOPK), ((0, 64),), -0.2, 0.2)), 0.05, 0.5)
    w_gate = normal_values(key_list[4], (EXPERTS, D, FF), D ** -0.5, 0.09375, ((0, 64), (1, 4)))
    w_up = normal_values(key_list[5], (EXPERTS, D, FF), D ** -0.5, 0.09375, ((0, 64), (1, 4)))
    w_down = normal_values(key_list[6], (EXPERTS, FF, D), FF ** -0.5, 0.21875, ((0, 64), (2, 4)))
    return dict(tokens=tokens, out_grad=out_grad, expert_ids=expert_ids, route_probs=route_probs, w_gate=w_gate, w_up=w_up, w_down=w_down)


def reference(tokens, out_grad, expert_ids, route_probs, w_gate, w_up, w_down):
    assigns = TOK_DEV * TOPK
    quarter = D // N_TP
    blocks = expert_ids.reshape(N_EP, assigns).astype(jnp.int32)
    onehot = (blocks[:, :, None] == jnp.arange(EXPERTS, dtype=jnp.int32)[None, None, :]).astype(jnp.int32)
    ranks = jnp.sum((jnp.cumsum(onehot, 1) - onehot) * onehot, 2).astype(jnp.int32)
    slots = (blocks * CAP + ranks).astype(jnp.int32)
    global_ids = (jnp.arange(N_EP, dtype=jnp.int32) * assigns)[:, None] + jnp.arange(assigns, dtype=jnp.int32)[None, :]

    def fill_row(slot_row, id_row):
        return jnp.full((EXPERTS * CAP,), TOKENS * TOPK, jnp.int32).at[slot_row].set(id_row)

    table = jax.vmap(fill_row)(slots, global_ids)
    table = table.reshape(N_EP, EXPERTS, CAP).transpose(1, 0, 2).reshape(EXPERTS, N_EP * CAP)
    padded_x = jnp.concatenate([tokens, jnp.zeros((1, D), tokens.dtype)], 0)
    padded_dy = jnp.concatenate([out_grad, jnp.zeros((1, D), out_grad.dtype)], 0)
    padded_p = jnp.concatenate([route_probs.reshape(-1), jnp.zeros((1,), jnp.float32)], 0)
    scale = 1.0 / TOK_DEV

    def expert_step(accum, inputs):
        e_table, gate_mat, up_mat, down_mat = inputs
        token_of = (e_table // TOPK).astype(jnp.int32)
        x_rows = padded_x[token_of]
        dy_rows = (padded_dy[token_of].astype(jnp.float32) * padded_p[e_table][:, None]).astype(jnp.bfloat16)
        x_quart = x_rows.astype(jnp.float32).reshape(-1, N_TP, quarter)
        dy_quart = dy_rows.astype(jnp.float32).reshape(-1, N_TP, quarter)
        gate = jnp.sum(jnp.einsum('sqd,qdf->qsf', x_quart, gate_mat.astype(jnp.float32).reshape(N_TP, quarter, FF)).astype(jnp.bfloat16).astype(jnp.float32), 0)
        up = jnp.sum(jnp.einsum('sqd,qdf->qsf', x_quart, up_mat.astype(jnp.float32).reshape(N_TP, quarter, FF)).astype(jnp.bfloat16).astype(jnp.float32), 0)
        dact = jnp.sum(jnp.einsum('sqd,fqd->qsf', dy_quart, down_mat.astype(jnp.float32).reshape(FF, N_TP, quarter)).astype(jnp.bfloat16).astype(jnp.float32), 0)
        sig = jax.nn.sigmoid(gate)
        act = (gate * sig * up).astype(jnp.bfloat16)
        dgate = (dact * up * sig * (1.0 + gate * (1.0 - sig))).astype(jnp.bfloat16)
        dup = (dact * gate * sig).astype(jnp.bfloat16)
        dx_rows = (jnp.dot(dgate, gate_mat.T, preferred_element_type=jnp.float32) + jnp.dot(dup, up_mat.T, preferred_element_type=jnp.float32)).astype(jnp.bfloat16)
        accum = accum.at[token_of].add(dx_rows.astype(jnp.float32))
        x_sq = jnp.square(x_rows.astype(jnp.float32)).astype(jnp.bfloat16)
        act_sq = jnp.square(act.astype(jnp.float32)).astype(jnp.bfloat16)
        dg_sq = jnp.square(dgate.astype(jnp.float32)).astype(jnp.bfloat16)
        du_sq = jnp.square(dup.astype(jnp.float32)).astype(jnp.bfloat16)
        dy_sq = jnp.square(dy_rows.astype(jnp.float32)).astype(jnp.bfloat16)
        fish_gate = (jnp.dot(x_sq.T, dg_sq, preferred_element_type=jnp.float32) * scale).astype(jnp.bfloat16)
        fish_up = (jnp.dot(x_sq.T, du_sq, preferred_element_type=jnp.float32) * scale).astype(jnp.bfloat16)
        fish_down = (jnp.dot(act_sq.T, dy_sq, preferred_element_type=jnp.float32) * scale).astype(jnp.bfloat16)
        return accum, (fish_gate, fish_up, fish_down)

    start = jnp.zeros((TOKENS + 1, D), jnp.float32)
    accum, outs = lax.scan(expert_step, start, (table, w_gate, w_up, w_down))
    grad_tokens = accum[:TOKENS].astype(jnp.bfloat16)
    return grad_tokens, outs[0], outs[1], outs[2]
```

```python
import functools

import jax
import jax.numpy as jnp
from jax import lax
from jax.experimental import pallas as pl
from jax.experimental.pallas import tpu as pltpu
from jax.sharding import PartitionSpec as P

BF = jnp.bfloat16
F32 = jnp.float32
GROUP = 8
META = 16
VMEM = 100 * 1024 * 1024 // 2
CHUNKS = ((0, -1, 1), (-2, 2), (-3, 3, 4))


def dot(left, right, dims):
    return lax.dot_general(left, right, ((dims[0], dims[1]), ((), ())), preferred_element_type=F32)


def call(body, outs, args, name, grid=(1,), in_specs=None, out_specs=None, prefetch=0, scratch=()):
    whole = lambda a: pl.BlockSpec(a.shape, lambda *_: (0,) * len(a.shape))
    ins = args[prefetch:]
    in_specs = [whole(a) if s is None else s for a, s in zip(ins, in_specs or [None] * len(ins))]
    out_specs = [whole(a) if s is None else s for a, s in zip(outs, out_specs or [None] * len(outs))]
    return pl.pallas_call(
        body,
        out_shape=outs,
        grid_spec=pltpu.PrefetchScalarGridSpec(
            num_scalar_prefetch=prefetch,
            grid=grid,
            in_specs=in_specs,
            out_specs=out_specs,
            scratch_shapes=scratch,
        ),
        compiler_params=pltpu.CompilerParams(
            dimension_semantics=("arbitrary",) * len(grid), vmem_limit_bytes=VMEM
        ),
        name=name,
    )(*args)


def payload_body(tok, grad, ids, probs, out):
    rows = tok.shape[0]
    out[0:rows, :] = tok[...]
    out[rows : 2 * rows, :] = grad[...]
    p = probs[...]
    high = p.astype(BF).astype(F32)
    mid = (p - high).astype(BF).astype(F32)
    low = p - high - mid
    pad = jnp.zeros((META - p.shape[0], p.shape[1]), F32)
    parts = [jnp.concatenate([v, pad], 0) for v in (ids[...].astype(F32), high, mid, low)]
    used = sum(v.shape[1] for v in parts)
    parts.append(jnp.zeros((META, out.shape[1] - used), F32))
    out[2 * rows :, :] = jnp.concatenate(parts, 1).astype(BF)


def pick_body(cap, place, *refs):
    pays, (send, pick) = refs[:-2], refs[-2:]
    count = len(pays)
    rows = (pays[0].shape[0] - META) // 2
    width = pays[0].shape[1]
    per = pick.shape[0] // GROUP
    first = place[0] // GROUP * GROUP
    before = (
        lax.broadcasted_iota(jnp.int32, (rows, rows), 0) < lax.broadcasted_iota(jnp.int32, (rows, rows), 1)
    ).astype(F32).astype(BF)
    expert = (lax.broadcasted_iota(jnp.int32, (GROUP, GROUP, rows), 0) + first).astype(F32)
    codes, probs = [], []
    for at, pay in enumerate(pays):
        meta = pay[2 * rows :, : 4 * rows].astype(F32)[:GROUP]
        ids, p = meta[:, :rows], meta[:, rows : 2 * rows] + meta[:, 2 * rows : 3 * rows] + meta[:, 3 * rows :]
        named = expert == ids[None]
        has = jnp.sum(jnp.where(named, 1.0, 0.0), 1)
        probs.append(jnp.sum(jnp.where(named, p[None], 0.0), 1))
        rank = dot(has.astype(BF), before, ((1,), (0,)))
        codes.append(jnp.where(has > 0.5, rank + 32.0 * at, -1.0))
    codes, probs = jnp.concatenate(codes, 1), jnp.concatenate(probs, 1)
    row = lax.broadcasted_iota(jnp.int32, (per, count * rows), 0)
    code = row
    for at in range(count):
        code = code + jnp.where(row >= cap * (at + 1), 32 - cap, 0)
    code = code.astype(F32)
    scales = []
    for d in range(GROUP):
        hit = code == codes[d : d + 1]
        pick[d * per : (d + 1) * per, :] = jnp.where(hit, 1.0, 0.0).astype(BF)
        scales.append(jnp.sum(jnp.where(hit, probs[d : d + 1], 0.0), 1, keepdims=True))
    onehot = pick[...]
    toks = jnp.concatenate([pay[0:rows, :] for pay in pays], 0)
    send[:, :width] = dot(onehot, toks, ((1,), (0,))).astype(BF)
    grads = jnp.concatenate([pay[rows : 2 * rows, :] for pay in pays], 0)
    send[:, width:] = (dot(onehot, grads, ((1,), (0,))) * jnp.concatenate(scales, 0)).astype(BF)


def partial_body(side, rows_ref, gate, up, down, send, keep, work):
    half = send.shape[1]
    width = gate.shape[1]
    kept = pl.multiple_of(side[0] * half, 16)
    sent = pl.multiple_of((1 - side[0]) * half, 16)
    for at in range(3):
        if at < 2:
            work[...] = dot(rows_ref[:, :width], (gate, up)[at][0], ((1,), (0,)))
        else:
            work[...] = dot(rows_ref[:, width:], down[0], ((1,), (1,)))
        send[at] = work[pl.ds(sent, half), :].astype(BF)
        keep[at] = work[pl.ds(kept, half), :].astype(BF)


def pair_body(side, keep, got, out):
    out[...] = (keep[...].astype(F32) + got[...].astype(F32)).astype(BF)


def back_body(side, keep, got, more, out):
    gate, up, dact = (keep[i].astype(F32) + got[i].astype(F32) + more[i].astype(F32) for i in range(3))
    sig = 1.0 / (1.0 + jnp.exp(-gate))
    out[0] = (gate * sig * up).astype(BF)
    out[1] = (dact * up * sig * (1.0 + gate * (1.0 - sig))).astype(BF)
    out[2] = (dact * gate * sig).astype(BF)


def input_body(side, own, near, far, last, gate, up, out, sq, work):
    quarter = own.shape[1]

    @pl.when(pl.program_id(0) == 0)
    def _():
        h, q = side[0], side[1]
        places = (2 * h + q, 2 * h + 1 - q, 2 * (1 - h) + q, 2 * (1 - h) + 1 - q)
        for place, ref in zip(places, (own, near, far, last)):
            at = pl.ds(pl.multiple_of(place * quarter, 16), quarter)
            for i in range(3):
                v = ref[i].astype(F32)
                sq[i, at, :] = (v * v).astype(BF)
                if i:
                    work[i - 1, at, :] = ref[i]

    out[...] = (dot(work[0], gate[0], ((1,), (1,))) + dot(work[1], up[0], ((1,), (1,)))).astype(BF)


def square_bf(values):
    v = values.astype(F32)
    return (v * v).astype(BF)


def fisher_body(scale, *refs):
    count = (len(refs) - 5) // 2
    rows, sqs = refs[:count], refs[count : 2 * count]
    f_gate, f_up, f_down, x_sq, dy_sq = refs[2 * count :]
    width = x_sq.shape[1]

    @pl.when(pl.program_id(0) == 0)
    def _():
        at = 0
        for ref in rows:
            x_sq[at : at + ref.shape[0], :] = square_bf(ref[:, :width])
            dy_sq[at : at + ref.shape[0], :] = square_bf(ref[:, width:])
            at += ref.shape[0]

    act, dgate, dup = (jnp.concatenate([s[i] for s in sqs], 0) for i in range(3))
    f_gate[0] = (dot(x_sq[...], dgate, ((0,), (0,))) * scale).astype(BF)
    f_up[0] = (dot(x_sq[...], dup, ((0,), (0,))) * scale).astype(BF)
    f_down[0] = (dot(act, dy_sq[...], ((0,), (0,))) * scale).astype(BF)


def combine_body(pick, got, *outs):
    rows = outs[0].shape[0]
    for at, out in enumerate(outs):
        out[...] = dot(pick[:, at * rows : (at + 1) * rows], got[...], ((0,), (0,))).astype(out.dtype)


def total_body(*refs):
    total = refs[0][...].astype(F32)
    for ref in refs[1:-1]:
        total = total + ref[...].astype(F32)
    refs[-1][...] = total.astype(BF)


def shape(dims, dtype=BF):
    return jax.ShapeDtypeStruct(dims, dtype)


def on_device(tokens, out_grad, expert_ids, route_probs, w_gate, w_up, w_down):
    rows, width = tokens.shape
    top = expert_ids.shape[1]
    ep, tp = lax.axis_size("ep"), lax.axis_size("tp")
    hidden = w_gate.shape[2]
    cap = rows * top * 9 // (8 * ep)
    deep = ep // GROUP
    groups = [[z * GROUP + i for i in range(GROUP)] for z in range(deep)]

    def along_z(value, step):
        n = ep * tp
        return lax.ppermute(value, ("ep", "tp"), [(i, (i + step * GROUP * tp) % n) for i in range(n)])

    def along_x(value, which):
        pairs = []
        for i in range(ep * tp):
            e, x = divmod(i, tp)
            pairs.append((i, e * tp + (x ^ 1 if (e % 2 == 0) == (which == 1) else 3 - x)))
        return lax.ppermute(value, ("ep", "tp"), pairs)

    def across(value):
        split = value.reshape(GROUP, -1, value.shape[1])
        return lax.all_to_all(
            split, "ep", split_axis=0, concat_axis=0, axis_index_groups=groups, tiled=True
        ).reshape(value.shape)

    e, x = lax.axis_index("ep"), lax.axis_index("tp")
    place = e.astype(jnp.int32).reshape(1)
    outer = (x ^ (x >> 1)) & 1
    upper = x >> 1
    even = e % 2 == 0
    side = jnp.stack([jnp.where(even, outer, upper), jnp.where(even, upper, outer)]).astype(jnp.int32)

    pays = {}
    (pays[0],) = call(
        payload_body,
        [shape((2 * rows + META, width))],
        [tokens, out_grad, expert_ids.T, route_probs.T],
        "payload",
    )
    for step in range(1, deep // 2):
        pays[-step] = along_z(pays[1 - step], 1)
        pays[step] = along_z(pays[step - 1], -1)
    pays[deep // 2] = along_z(pays[1 - deep // 2], 1)

    tile = 256
    steps = hidden // tile
    picks, recvs, sqs, parts = [], [], [], []
    for offsets in CHUNKS:
        count = len(offsets)
        per = -(-count * cap // 8) * 8
        total = GROUP * per
        half, quarter = total // 2, total // 4
        send, pick = call(
            functools.partial(pick_body, cap),
            [shape((total, 2 * width)), shape((total, count * rows))],
            [place] + [pays[o] for o in offsets],
            "pick",
            prefetch=1,
        )
        recv = across(send)
        w_in = pl.BlockSpec((1, width, tile), lambda j, s: (0, 0, j))
        half_out = pl.BlockSpec((3, half, tile), lambda j, s: (0, 0, j))
        give, keep = call(
            partial_body,
            [shape((3, half, hidden))] * 2,
            [side, recv, w_gate, w_up, w_down],
            "partial",
            grid=(steps,),
            in_specs=[None, w_in, w_in, pl.BlockSpec((1, tile, width), lambda j, s: (0, j, 0))],
            out_specs=[half_out, half_out],
            prefetch=1,
            scratch=[pltpu.VMEM((total, tile), F32)],
        )
        got = along_x(give, 1)
        theirs = pl.BlockSpec((3, quarter, hidden), lambda j, s: (0, 1 - s[1], 0))
        mine = pl.BlockSpec((3, quarter, hidden), lambda j, s: (0, s[1], 0))
        quarters = shape((3, quarter, hidden))
        (give,) = call(pair_body, [quarters], [side, keep, got], "pair", in_specs=[theirs, theirs], prefetch=1)
        more = along_x(give, 2)
        (own,) = call(
            back_body, [quarters], [side, keep, got, more], "back", in_specs=[mine, mine, None], prefetch=1
        )
        near = along_x(own, 2)
        far = along_x(own, 1)
        last = along_x(near, 1)
        w_out = pl.BlockSpec((1, tile, hidden), lambda j, s: (0, j, 0))
        d_rows, sq = call(
            input_body,
            [shape((total, width)), shape((3, total, hidden))],
            [side, own, near, far, last, w_gate, w_up],
            "input_grad",
            grid=(width // tile,),
            in_specs=[None] * 4 + [w_out, w_out],
            out_specs=[pl.BlockSpec((total, tile), lambda j, s: (0, j)), None],
            prefetch=1,
            scratch=[pltpu.VMEM((2, total, hidden), BF)],
        )
        back = across(d_rows)
        sums = call(
            combine_body,
            [shape((rows, width), BF if o else F32) for o in offsets],
            [pick, back],
            "combine",
        )
        for o, s in zip(offsets, sums):
            parts.append(along_z(s, o) if o else s)
        recvs.append(recv)
        sqs.append(sq)
    (grad_tokens,) = call(total_body, [shape((rows, width))], parts, "total")
    every = sum(r.shape[0] for r in recvs)
    f_in = pl.BlockSpec((1, width, tile), lambda j: (0, 0, j))
    fishers = call(
        functools.partial(fisher_body, 1.0 / rows),
        [shape((1, width, hidden)), shape((1, width, hidden)), shape((1, hidden, width))],
        recvs + sqs,
        "fisher",
        grid=(steps,),
        in_specs=[None] * len(recvs)
        + [pl.BlockSpec((3, s.shape[1], tile), lambda j: (0, 0, j)) for s in sqs],
        out_specs=[f_in, f_in, pl.BlockSpec((1, tile, width), lambda j: (0, j, 0))],
        scratch=[pltpu.VMEM((every, width), BF)] * 2,
    )
    return (grad_tokens, *fishers)


def solution(mesh):
    in_specs = (
        P("ep", "tp"),
        P("ep", "tp"),
        P("ep", None),
        P("ep", None),
        P("ep", "tp", None),
        P("ep", "tp", None),
        P("ep", None, "tp"),
    )
    out_specs = (P("ep", "tp"), P("ep", "tp", None), P("ep", "tp", None), P("ep", None, "tp"))
    return jax.shard_map(
        on_device, mesh=mesh, in_specs=in_specs, out_specs=out_specs, check_vma=False
    )
```

```python
import functools

import jax
import jax.numpy as jnp
from jax import lax
from jax.experimental import pallas as pl
from jax.experimental.pallas import tpu as pltpu
from jax.sharding import PartitionSpec as P

BF = jnp.bfloat16
F32 = jnp.float32
GROUP = 8
META = 16
COSTS = {'payload': 13284000, 'pick': 35424000, 'partial': 88560000, 'pair': 20664000, 'back': 25092000, 'input_grad': 88560000, 'combine': 18450000, 'fisher': 165312000, 'total': 29520000}
VMEM = 100 * 1024 * 1024 // 2
CHUNKS = ((0, -1, 1), (-2, 2), (-3, 3, 4))

ORDER = (
    ('ring', 2),
    ('pick', 0),
    ('ring', 3),
    ('pick', 1),
    ('partial', 0),
    ('ring', 4),
    ('partial', 1),
    ('pick', 2),
    ('pair', 0),
    ('back', 0),
    ('pair', 1),
    ('partial', 2),
    ('back', 1),
    ('pair', 2),
    ('input', 0),
    ('back', 2),
    ('input', 1),
    ('combine', 0),
    ('input', 2),
    ('combine', 1),
    ('total', False),
    ('combine', 2),
    ('fisher', 0),
    ('total', True),
)


def dot(left, right, dims):
    return lax.dot_general(left, right, ((dims[0], dims[1]), ((), ())), preferred_element_type=F32)


def call(body, outs, args, name, grid=(1,), in_specs=None, out_specs=None, prefetch=0, scratch=()):
    whole = lambda a: pl.BlockSpec(a.shape, lambda *_: (0,) * len(a.shape))
    ins = args[prefetch:]
    in_specs = [whole(a) if s is None else s for a, s in zip(ins, in_specs or [None] * len(ins))]
    out_specs = [whole(a) if s is None else s for a, s in zip(outs, out_specs or [None] * len(outs))]
    args = list(args[:prefetch]) + list(ins)
    return pl.pallas_call(
        body,
        out_shape=[pltpu.HBM(o.shape, o.dtype) for o in outs],
        grid_spec=pltpu.PrefetchScalarGridSpec(
            num_scalar_prefetch=prefetch,
            grid=grid,
            in_specs=in_specs,
            out_specs=out_specs,
            scratch_shapes=scratch,
        ),
        compiler_params=pltpu.CompilerParams(
            dimension_semantics=("arbitrary",) * len(grid), vmem_limit_bytes=VMEM
        ),
        cost_estimate=pl.CostEstimate(flops=COSTS[name] * 300, bytes_accessed=1, transcendentals=0),
        name=name,
    )(*args)


def payload_body(tok, grad, ids, probs, out):
    rows = tok.shape[0]
    out[0:rows, :] = tok[...]
    out[rows : 2 * rows, :] = grad[...]
    p = probs[...]
    high = p.astype(BF).astype(F32)
    mid = (p - high).astype(BF).astype(F32)
    low = p - high - mid
    pad = jnp.zeros((META - p.shape[0], p.shape[1]), F32)
    parts = [jnp.concatenate([v, pad], 0) for v in (ids[...].astype(F32), high, mid, low)]
    used = sum(v.shape[1] for v in parts)
    parts.append(jnp.zeros((META, out.shape[1] - used), F32))
    out[2 * rows :, :] = jnp.concatenate(parts, 1).astype(BF)


def pick_body(cap, place, *refs):
    pays, (send, pick) = refs[:-2], refs[-2:]
    count = len(pays)
    rows = (pays[0].shape[0] - META) // 2
    width = pays[0].shape[1]
    per = pick.shape[0] // GROUP
    first = place[0] // GROUP * GROUP
    before = (
        lax.broadcasted_iota(jnp.int32, (rows, rows), 0) < lax.broadcasted_iota(jnp.int32, (rows, rows), 1)
    ).astype(F32).astype(BF)
    expert = (lax.broadcasted_iota(jnp.int32, (GROUP, GROUP, rows), 0) + first).astype(F32)
    codes, probs = [], []
    for at, pay in enumerate(pays):
        meta = pay[2 * rows :, : 4 * rows].astype(F32)[:GROUP]
        ids, p = meta[:, :rows], meta[:, rows : 2 * rows] + meta[:, 2 * rows : 3 * rows] + meta[:, 3 * rows :]
        named = expert == ids[None]
        has = jnp.sum(jnp.where(named, 1.0, 0.0), 1)
        probs.append(jnp.sum(jnp.where(named, p[None], 0.0), 1))
        rank = dot(has.astype(BF), before, ((1,), (0,)))
        codes.append(jnp.where(has > 0.5, rank + 32.0 * at, -1.0))
    codes, probs = jnp.concatenate(codes, 1), jnp.concatenate(probs, 1)
    row = lax.broadcasted_iota(jnp.int32, (per, count * rows), 0)
    code = row
    for at in range(count):
        code = code + jnp.where(row >= cap * (at + 1), 32 - cap, 0)
    code = code.astype(F32)
    scales = []
    for d in range(GROUP):
        hit = code == codes[d : d + 1]
        pick[d * per : (d + 1) * per, :] = jnp.where(hit, 1.0, 0.0).astype(BF)
        scales.append(jnp.sum(jnp.where(hit, probs[d : d + 1], 0.0), 1, keepdims=True))
    onehot = pick[...]
    toks = jnp.concatenate([pay[0:rows, :] for pay in pays], 0)
    send[:, :width] = dot(onehot, toks, ((1,), (0,))).astype(BF)
    grads = jnp.concatenate([pay[rows : 2 * rows, :] for pay in pays], 0)
    send[:, width:] = (dot(onehot, grads, ((1,), (0,))) * jnp.concatenate(scales, 0)).astype(BF)


def partial_body(side, rows_ref, gate, up, down, send, keep, work):
    half = send.shape[1]
    width = gate.shape[1]
    kept = pl.multiple_of(side[0] * half, 16)
    sent = pl.multiple_of((1 - side[0]) * half, 16)
    for at in range(3):
        if at < 2:
            work[...] = dot(rows_ref[:, :width], (gate, up)[at][0], ((1,), (0,)))
        else:
            work[...] = dot(rows_ref[:, width:], down[0], ((1,), (1,)))
        send[at] = work[pl.ds(sent, half), :].astype(BF)
        keep[at] = work[pl.ds(kept, half), :].astype(BF)


def pair_body(side, keep, got, out):
    out[...] = (keep[...].astype(F32) + got[...].astype(F32)).astype(BF)


def swiglu_back(gate, up, dact):
    sig = 1.0 / (1.0 + jnp.exp(-gate))
    act = gate * sig * up
    dgate = dact * up * sig * (1.0 + gate * (1.0 - sig))
    return act.astype(BF), dgate.astype(BF), (dact * gate * sig).astype(BF)


def back_body(side, keep, got, more, out):
    sums = (keep[i].astype(F32) + got[i].astype(F32) + more[i].astype(F32) for i in range(3))
    out[0], out[1], out[2] = swiglu_back(*sums)


def places_of(side):
    h, q = side[0], side[1]
    return 2 * h + q, 2 * h + 1 - q, 2 * (1 - h) + q, 2 * (1 - h) + 1 - q


def input_body(side, own, near, far, last, gate, up, out, work):
    quarter = own.shape[1]

    @pl.when(pl.program_id(0) == 0)
    def _():
        for place, ref in zip(places_of(side), (own, near, far, last)):
            at = pl.ds(pl.multiple_of(place * quarter, 16), quarter)
            work[0, at, :] = ref[1]
            work[1, at, :] = ref[2]

    out[...] = (dot(work[0], gate[0], ((1,), (1,))) + dot(work[1], up[0], ((1,), (1,)))).astype(BF)


def square_bf(values):
    v = values.astype(F32)
    return (v * v).astype(BF)


def fisher_body(scale, cuts, side, *refs):
    grads, rows = refs[: sum(cuts)], refs[sum(cuts) : sum(cuts) + len(cuts)]
    f_gate, f_up, f_down, x_sq, dy_sq = refs[sum(cuts) + len(cuts) :]
    width = x_sq.shape[1]

    @pl.when(pl.program_id(0) == 0)
    def _():
        at = 0
        for ref, cut in zip(rows, cuts):
            part = ref.shape[0] // cut
            for place in places_of(side) if cut > 1 else (0,):
                values = ref[pl.ds(pl.multiple_of(place * part, 16), part), :]
                x_sq[at : at + part, :] = square_bf(values[:, :width])
                dy_sq[at : at + part, :] = square_bf(values[:, width:])
                at += part

    act, dgate, dup = (jnp.concatenate([square_bf(g[i]) for g in grads], 0) for i in range(3))
    f_gate[0] = (dot(x_sq[...], dgate, ((0,), (0,))) * scale).astype(BF)
    f_up[0] = (dot(x_sq[...], dup, ((0,), (0,))) * scale).astype(BF)
    f_down[0] = (dot(act, dy_sq[...], ((0,), (0,))) * scale).astype(BF)


def combine_body(pick, got, *outs):
    rows = outs[0].shape[0]
    for at, out in enumerate(outs):
        out[...] = dot(pick[:, at * rows : (at + 1) * rows], got[...], ((0,), (0,))).astype(out.dtype)


def total_body(*refs):
    total = refs[0][...].astype(F32)
    for ref in refs[1:-1]:
        total = total + ref[...].astype(F32)
    refs[-1][...] = total.astype(refs[-1].dtype)


def shape(dims, dtype=BF):
    return jax.ShapeDtypeStruct(dims, dtype)


def on_device(tokens, out_grad, expert_ids, route_probs, w_gate, w_up, w_down):
    rows, width = tokens.shape
    top = expert_ids.shape[1]
    ep, tp = lax.axis_size("ep"), lax.axis_size("tp")
    hidden = w_gate.shape[2]
    cap = rows * top * 9 // (8 * ep)
    deep = ep // GROUP
    groups = [[z * GROUP + i for i in range(GROUP)] for z in range(deep)]

    def along_z(value, step):
        n = ep * tp
        return lax.ppermute(value, ("ep", "tp"), [(i, (i + step * GROUP * tp) % n) for i in range(n)])

    def along_x(value, which):
        pairs = []
        for i in range(ep * tp):
            e, x = divmod(i, tp)
            pairs.append((i, e * tp + (x ^ 1 if (e % 2 == 0) == (which == 1) else 3 - x)))
        return lax.ppermute(value, ("ep", "tp"), pairs)

    def across(value):
        split = value.reshape(GROUP, -1, value.shape[1])
        return lax.all_to_all(
            split, "ep", split_axis=0, concat_axis=0, axis_index_groups=groups, tiled=True
        ).reshape(value.shape)

    e, x = lax.axis_index("ep"), lax.axis_index("tp")
    place = e.astype(jnp.int32).reshape(1)
    outer = (x ^ (x >> 1)) & 1
    upper = x >> 1
    even = e % 2 == 0
    side = jnp.stack([jnp.where(even, outer, upper), jnp.where(even, upper, outer)]).astype(jnp.int32)

    pays = {}
    (pays[0],) = call(
        payload_body,
        [shape((2 * rows + META, width))],
        [tokens, out_grad, expert_ids.T, route_probs.T],
        "payload",
    )
    pays[-1], pays[1] = along_z(pays[0], 1), along_z(pays[0], -1)

    tile = 256
    steps = hidden // tile
    last = [pays[0]]

    def run(body, outs, args, name, **kw):
        at = kw.get("prefetch", 0)
        args = list(args)
        args[at], _ = lax.optimization_barrier((args[at], last[0]))
        outs = call(body, outs, args, name, **kw)
        last[0] = outs[0]
        return outs

    made = [{} for _ in CHUNKS]

    def dims(k):
        count = len(CHUNKS[k])
        per = -(-count * cap // 8) * 8
        return count, GROUP * per, GROUP * per // 2, GROUP * per // 4

    def ring(step):
        for sign in (-1, 1):
            if step < deep // 2 or sign < 0:
                value, _ = lax.optimization_barrier((pays[sign * (step - 1)], last[0]))
                pays[sign * step if step < deep // 2 else step] = along_z(value, -sign)

    def pick(k):
        count, total, _, _ = dims(k)
        send, made[k]["pick"] = run(
            functools.partial(pick_body, cap),
            [shape((total, 2 * width)), shape((total, count * rows))],
            [place] + [pays[o] for o in CHUNKS[k]],
            "pick",
            prefetch=1,
        )
        made[k]["recv"] = across(send)

    def partial(k):
        _, total, half, _ = dims(k)
        w_in = pl.BlockSpec((1, width, tile), lambda j, s: (0, 0, j))
        half_out = pl.BlockSpec((3, half, tile), lambda j, s: (0, 0, j))
        give, made[k]["keep"] = run(
            partial_body,
            [shape((3, half, hidden))] * 2,
            [side, made[k]["recv"], w_gate, w_up, w_down],
            "partial",
            grid=(steps,),
            in_specs=[None, w_in, w_in, pl.BlockSpec((1, tile, width), lambda j, s: (0, j, 0))],
            out_specs=[half_out, half_out],
            prefetch=1,
            scratch=[pltpu.VMEM((total, tile), F32)],
        )
        made[k]["got"] = along_x(give, 1)

    def pair(k):
        quarter = dims(k)[3]
        theirs = pl.BlockSpec((3, quarter, hidden), lambda j, s: (0, 1 - s[1], 0))
        (give,) = run(
            pair_body,
            [shape((3, quarter, hidden))],
            [side, made[k]["keep"], made[k]["got"]],
            "pair",
            in_specs=[theirs, theirs],
            prefetch=1,
        )
        made[k]["more"] = along_x(give, 2)

    def back(k):
        quarter = dims(k)[3]
        mine = pl.BlockSpec((3, quarter, hidden), lambda j, s: (0, s[1], 0))
        (own,) = run(
            back_body,
            [shape((3, quarter, hidden))],
            [side, made[k]["keep"], made[k]["got"], made[k]["more"]],
            "back",
            in_specs=[mine, mine, None],
            prefetch=1,
        )
        near = along_x(own, 2)
        made[k]["all"] = [own, near, along_x(own, 1), along_x(near, 1)]

    def input_grad(k):
        _, total, _, _ = dims(k)
        w_out = pl.BlockSpec((1, tile, hidden), lambda j, s: (0, j, 0))
        (d_rows,) = run(
            input_body,
            [shape((total, width))],
            [side] + made[k]["all"] + [w_gate, w_up],
            "input_grad",
            grid=(width // tile,),
            in_specs=[None] * 4 + [w_out, w_out],
            out_specs=[pl.BlockSpec((total, tile), lambda j, s: (0, j))],
            prefetch=1,
            scratch=[pltpu.VMEM((2, total, hidden), BF)],
        )
        made[k]["back"] = across(d_rows)

    def combine(k):
        sums = run(
            combine_body,
            [shape((rows, width), BF if o else F32) for o in CHUNKS[k]],
            [made[k]["pick"], made[k]["back"]],
            "combine",
        )
        made[k]["sums"] = [along_z(s, o) if o else s for o, s in zip(CHUNKS[k], sums)]

    def fisher(_):
        recvs, grads = [m["recv"] for m in made], [g for m in made for g in m["all"]]
        every = sum(r.shape[0] for r in recvs)
        f_in = pl.BlockSpec((1, width, tile), lambda j, s: (0, 0, j))
        fishers.extend(
            run(
                functools.partial(fisher_body, 1.0 / rows, [len(m["all"]) for m in made]),
                [shape((1, width, hidden)), shape((1, width, hidden)), shape((1, hidden, width))],
                [side] + grads + recvs,
                "fisher",
                grid=(steps,),
                in_specs=[pl.BlockSpec((3, g.shape[1], tile), lambda j, s: (0, 0, j)) for g in grads]
                + [None] * len(recvs),
                out_specs=[f_in, f_in, pl.BlockSpec((1, tile, width), lambda j, s: (0, j, 0))],
                prefetch=1,
                scratch=[pltpu.VMEM((every, width), BF)] * 2,
            )
        )

    def total(last_one):
        parts = held + [p for m in made for p in m.pop("sums", [])]
        held[:] = run(total_body, [shape((rows, width), BF if last_one else F32)], parts, "total")

    fishers, held = [], []
    steps_of = {
        "pick": pick, "partial": partial, "pair": pair, "back": back, "input": input_grad, "combine": combine, "fisher": fisher, "total": total, "ring": ring,
    }
    for step, k in ORDER:
        steps_of[step](k)
    return (held[0], *fishers)


def solution(mesh):
    in_specs = (
        P("ep", "tp"),
        P("ep", "tp"),
        P("ep", None),
        P("ep", None),
        P("ep", "tp", None),
        P("ep", "tp", None),
        P("ep", None, "tp"),
    )
    out_specs = (P("ep", "tp"), P("ep", "tp", None), P("ep", "tp", None), P("ep", None, "tp"))
    return jax.shard_map(
        on_device, mesh=mesh, in_specs=in_specs, out_specs=out_specs, check_vma=False
    )
```

```python
import functools

import jax
import jax.numpy as jnp
from jax import lax
from jax.experimental import pallas as pl
from jax.experimental.pallas import tpu as pltpu
from jax.sharding import PartitionSpec as P

BF = jnp.bfloat16
F32 = jnp.float32
GROUP = 8
META = 16
COSTS = {'payload': 33210000, 'pick': 88560000, 'partial': 22140000, 'pair': 51660000, 'back': 62730000, 'input_grad': 221400000, 'combine': 46125000, 'fisher': 413280000, 'total': 73800000}
VMEM = 100 * 1024 * 1024 // 2
CHUNKS = ([0, -1, 1], [-2, 2], [-3, 3, 4])

ORDER = (
    ('ring', 2),
    ('ring', 3),
    ('ring', 4),
    ('pick', 0),
    ('pick', 1),
    ('partial', 0),
    ('partial', 1),
    ('pick', 2),
    ('pair', 0),
    ('pair', 1),
    ('back', 0),
    ('partial', 2),
    ('input', 0),
    ('back', 1),
    ('pair', 2),
    ('back', 2),
    ('combine', 0),
    ('input', 1),
    ('input', 2),
    ('combine', 1),
    ('combine', 2),
    ('fisher', 0),
    ('total', False),
    ('total', True),
)


def dot(left, right, dims):
    return lax.dot_general(left, right, ((dims[0], dims[1]), ((), ())), preferred_element_type=F32)


def call(body, outs, args, name, grid=(1,), in_specs=None, out_specs=None, prefetch=0, scratch=()):
    whole = lambda a: pl.BlockSpec(a.shape, lambda *_: (0,) * len(a.shape))
    ins = args[prefetch:]
    in_specs = [whole(a) if s is None else s for a, s in zip(ins, in_specs or [None] * len(ins))]
    out_specs = [whole(a) if s is None else s for a, s in zip(outs, out_specs or [None] * len(outs))]
    args = list(args[:prefetch]) + list(ins)
    return pl.pallas_call(
        body,
        out_shape=[pltpu.HBM(o.shape, o.dtype) for o in outs],
        grid_spec=pltpu.PrefetchScalarGridSpec(
            num_scalar_prefetch=prefetch,
            grid=grid,
            in_specs=in_specs,
            out_specs=out_specs,
            scratch_shapes=scratch,
        ),
        compiler_params=pltpu.CompilerParams(
            dimension_semantics=("arbitrary",) * len(grid), vmem_limit_bytes=VMEM
        ),
        cost_estimate=pl.CostEstimate(flops=COSTS[name] * 300, bytes_accessed=1, transcendentals=0),
        name=name,
    )(*args)


def payload_body(tok, grad, ids, probs, out):
    rows = tok.shape[0]
    out[0:rows, :] = tok[...]
    out[rows : 2 * rows, :] = grad[...]
    p = probs[...]
    high = p.astype(BF).astype(F32)
    mid = (p - high).astype(BF).astype(F32)
    low = p - high - mid
    pad = jnp.zeros((META - p.shape[0], p.shape[1]), F32)
    parts = [jnp.concatenate([v, pad], 0) for v in (ids[...].astype(F32), high, mid, low)]
    used = sum(v.shape[1] for v in parts)
    parts.append(jnp.zeros((META, out.shape[1] - used), F32))
    out[2 * rows :, :] = jnp.concatenate(parts, 1).astype(BF)


def pick_body(cap, place, *refs):
    pays, (send, pick) = refs[:-2], refs[-2:]
    count = len(pays)
    rows = (pays[0].shape[0] - META) // 2
    width = pays[0].shape[1]
    per = pick.shape[0] // GROUP
    first = place[0] // GROUP * GROUP
    before = (
        lax.broadcasted_iota(jnp.int32, (rows, rows), 0) < lax.broadcasted_iota(jnp.int32, (rows, rows), 1)
    ).astype(F32).astype(BF)
    expert = (lax.broadcasted_iota(jnp.int32, (GROUP, GROUP, rows), 0) + first).astype(F32)
    codes, probs = [], []
    for at, pay in enumerate(pays):
        meta = pay[2 * rows :, : 4 * rows].astype(F32)[:GROUP]
        ids, p = meta[:, :rows], meta[:, rows : 2 * rows] + meta[:, 2 * rows : 3 * rows] + meta[:, 3 * rows :]
        named = expert == ids[None]
        has = jnp.sum(jnp.where(named, 1.0, 0.0), 1)
        probs.append(jnp.sum(jnp.where(named, p[None], 0.0), 1))
        rank = dot(has.astype(BF), before, ((1,), (0,)))
        codes.append(jnp.where(has > 0.5, rank + 32.0 * at, -1.0))
    codes, probs = jnp.concatenate(codes, 1), jnp.concatenate(probs, 1)
    row = lax.broadcasted_iota(jnp.int32, (per, count * rows), 0)
    code = row
    for at in range(count):
        code = code + jnp.where(row >= cap * (at + 1), 32 - cap, 0)
    code = code.astype(F32)
    scales = []
    for d in range(GROUP):
        hit = code == codes[d : d + 1]
        pick[d * per : (d + 1) * per, :] = jnp.where(hit, 1.0, 0.0).astype(BF)
        scales.append(jnp.sum(jnp.where(hit, probs[d : d + 1], 0.0), 1, keepdims=True))
    onehot = pick[...]
    toks = jnp.concatenate([pay[0:rows, :] for pay in pays], 0)
    send[:, :width] = dot(onehot, toks, ((1,), (0,))).astype(BF)
    grads = jnp.concatenate([pay[rows : 2 * rows, :] for pay in pays], 0)
    send[:, width:] = (dot(onehot, grads, ((1,), (0,))) * jnp.concatenate(scales, 0)).astype(BF)


def partial_body(side, rows_ref, gate, up, down, send, keep, work):
    half = send.shape[1]
    width = gate.shape[1]
    kept = pl.multiple_of(side[0] * half, 16)
    sent = pl.multiple_of((1 - side[0]) * half, 16)
    for at in range(3):
        if at < 2:
            work[...] = dot(rows_ref[:, :width], (gate, up)[at][0], ((1,), (0,)))
        else:
            work[...] = dot(rows_ref[:, width:], down[0], ((1,), (1,)))
        send[at] = work[pl.ds(sent, half), :].astype(BF)
        keep[at] = work[pl.ds(kept, half), :].astype(BF)


def pair_body(side, keep, got, out):
    out[...] = (keep[...].astype(F32) + got[...].astype(F32)).astype(BF)


def swiglu_back(gate, up, dact):
    sig = 1.0 / (1.0 + jnp.exp(-gate))
    act = gate * sig * up
    dgate = dact * up * sig * (1.0 + gate * (1.0 - sig))
    return act.astype(BF), dgate.astype(BF), (dact * gate * sig).astype(BF)


def back_body(side, keep, got, more, out):
    sums = (keep[i].astype(F32) + got[i].astype(F32) + more[i].astype(F32) for i in range(3))
    out[0], out[1], out[2] = swiglu_back(*sums)


def places_of(side):
    h, q = side[0], side[1]
    return 2 * h + q, 2 * h + 1 - q, 2 * (1 - h) + q, 2 * (1 - h) + 1 - q


def input_body(side, own, near, far, last, gate, up, out, work):
    quarter = own.shape[1]

    @pl.when(pl.program_id(0) == 0)
    def _():
        for place, ref in zip(places_of(side), (own, near, far, last)):
            at = pl.ds(pl.multiple_of(place * quarter, 16), quarter)
            work[0, at, :] = ref[1]
            work[1, at, :] = ref[2]

    out[...] = (dot(work[0], gate[0], ((1,), (1,))) + dot(work[1], up[0], ((1,), (1,)))).astype(BF)


def square_bf(values):
    v = values.astype(F32)
    return (v * v).astype(BF)


def fisher_body(scale, cuts, side, *refs):
    grads, rows = refs[: sum(cuts)], refs[sum(cuts) : sum(cuts) + len(cuts)]
    f_gate, f_up, f_down, x_sq, dy_sq = refs[sum(cuts) + len(cuts) :]
    width = x_sq.shape[1]

    @pl.when(pl.program_id(0) == 0)
    def _():
        at = 0
        for ref, cut in zip(rows, cuts):
            part = ref.shape[0] // cut
            for place in places_of(side) if cut > 1 else (0,):
                values = ref[pl.ds(pl.multiple_of(place * part, 16), part), :]
                x_sq[at : at + part, :] = square_bf(values[:, :width])
                dy_sq[at : at + part, :] = square_bf(values[:, width:])
                at += part

    act, dgate, dup = (jnp.concatenate([square_bf(g[i]) for g in grads], 0) for i in range(3))
    f_gate[0] = (dot(x_sq[...], dgate, ((0,), (0,))) * scale).astype(BF)
    f_up[0] = (dot(x_sq[...], dup, ((0,), (0,))) * scale).astype(BF)
    f_down[0] = (dot(act, dy_sq[...], ((0,), (0,))) * scale).astype(BF)


def combine_body(pick, got, *outs):
    rows = outs[0].shape[0]
    for at, out in enumerate(outs):
        out[...] = dot(pick[:, at * rows : (at + 1) * rows], got[...], ((0,), (0,))).astype(out.dtype)


def total_body(*refs):
    total = refs[0][...].astype(F32)
    for ref in refs[1:-1]:
        total = total + ref[...].astype(F32)
    refs[-1][...] = total.astype(refs[-1].dtype)


def shape(dims, dtype=BF):
    return jax.ShapeDtypeStruct(dims, dtype)


def on_device(tokens, out_grad, expert_ids, route_probs, w_gate, w_up, w_down):
    rows, width = tokens.shape
    top = expert_ids.shape[1]
    ep, tp = lax.axis_size("ep"), lax.axis_size("tp")
    hidden = w_gate.shape[2]
    cap = rows * top * 9 // (8 * ep)
    deep = ep // GROUP
    groups = [[z * GROUP + i for i in range(GROUP)] for z in range(deep)]

    def along_z(value, step):
        n = ep * tp
        return lax.ppermute(value, ("ep", "tp"), [(i, (i + step * GROUP * tp) % n) for i in range(n)])

    def along_x(value, which):
        pairs = []
        for i in range(ep * tp):
            e, x = divmod(i, tp)
            pairs.append((i, e * tp + (x ^ 1 if (e % 2 == 0) == (which == 1) else 3 - x)))
        return lax.ppermute(value, ("ep", "tp"), pairs)

    def across(value):
        split = value.reshape(GROUP, -1, value.shape[1])
        return lax.all_to_all(
            split, "ep", split_axis=0, concat_axis=0, axis_index_groups=groups, tiled=True
        ).reshape(value.shape)

    e, x = lax.axis_index("ep"), lax.axis_index("tp")
    place = e.astype(jnp.int32).reshape(1)
    outer = (x ^ (x >> 1)) & 1
    upper = x >> 1
    even = e % 2 == 0
    side = jnp.stack([jnp.where(even, outer, upper), jnp.where(even, upper, outer)]).astype(jnp.int32)

    pays = {}
    (pays[0],) = call(
        payload_body,
        [shape((2 * rows + META, width))],
        [tokens, out_grad, expert_ids.T, route_probs.T],
        "payload",
    )
    pays[-1], pays[1] = along_z(pays[0], 1), along_z(pays[0], -1)

    tile = 256
    steps = hidden // tile
    last = [pays[0]]

    def run(body, outs, args, name, **kw):
        at = kw.get("prefetch", 0)
        args = list(args)
        args[at], _ = lax.optimization_barrier((args[at], last[0]))
        outs = call(body, outs, args, name, **kw)
        last[0] = outs[0]
        return outs

    made = [{} for _ in CHUNKS]

    def dims(k):
        count = len(CHUNKS[k])
        per = -(-count * cap // 8) * 8
        return count, GROUP * per, GROUP * per // 2, GROUP * per // 4

    def ring(step):
        for sign in (-1, 1):
            if step < deep // 2 or sign < 0:
                value, _ = lax.optimization_barrier((pays[sign * (step - 1)], last[0]))
                pays[sign * step if step < deep // 2 else step] = along_z(value, -sign)

    def pick(k):
        count, total, _, _ = dims(k)
        send, made[k]["pick"] = run(
            functools.partial(pick_body, cap),
            [shape((total, 2 * width)), shape((total, count * rows))],
            [place] + [pays[o] for o in CHUNKS[k]],
            "pick",
            prefetch=1,
        )
        made[k]["recv"] = across(send)

    def partial(k):
        _, total, half, _ = dims(k)
        w_in = pl.BlockSpec((1, width, tile), lambda j, s: (0, 0, j))
        half_out = pl.BlockSpec((3, half, tile), lambda j, s: (0, 0, j))
        give, made[k]["keep"] = run(
            partial_body,
            [shape((3, half, hidden))] * 2,
            [side, made[k]["recv"], w_gate, w_up, w_down],
            "partial",
            grid=(steps,),
            in_specs=[None, w_in, w_in, pl.BlockSpec((1, tile, width), lambda j, s: (0, j, 0))],
            out_specs=[half_out, half_out],
            prefetch=1,
            scratch=[pltpu.VMEM((total, tile), F32)],
        )
        made[k]["got"] = along_x(give, 1)

    def pair(k):
        quarter = dims(k)[3]
        theirs = pl.BlockSpec((3, quarter, hidden), lambda j, s: (0, 1 - s[1], 0))
        (give,) = run(
            pair_body,
            [shape((3, quarter, hidden))],
            [side, made[k]["keep"], made[k]["got"]],
            "pair",
            in_specs=[theirs, theirs],
            prefetch=1,
        )
        made[k]["more"] = along_x(give, 2)

    def back(k):
        quarter = dims(k)[3]
        mine = pl.BlockSpec((3, quarter, hidden), lambda j, s: (0, s[1], 0))
        (own,) = run(
            back_body,
            [shape((3, quarter, hidden))],
            [side, made[k]["keep"], made[k]["got"], made[k]["more"]],
            "back",
            in_specs=[mine, mine, None],
            prefetch=1,
        )
        near = along_x(own, 2)
        made[k]["all"] = [own, near, along_x(own, 1), along_x(near, 1)]

    def input_grad(k):
        _, total, _, _ = dims(k)
        w_out = pl.BlockSpec((1, tile, hidden), lambda j, s: (0, j, 0))
        (d_rows,) = run(
            input_body,
            [shape((total, width))],
            [side] + made[k]["all"] + [w_gate, w_up],
            "input_grad",
            grid=(width // tile,),
            in_specs=[None] * 4 + [w_out, w_out],
            out_specs=[pl.BlockSpec((total, tile), lambda j, s: (0, j))],
            prefetch=1,
            scratch=[pltpu.VMEM((2, total, hidden), BF)],
        )
        made[k]["back"] = across(d_rows)

    def combine(k):
        sums = run(
            combine_body,
            [shape((rows, width), BF if o else F32) for o in CHUNKS[k]],
            [made[k]["pick"], made[k]["back"]],
            "combine",
        )
        made[k]["sums"] = [along_z(s, o) if o else s for o, s in zip(CHUNKS[k], sums)]

    def fisher(_):
        recvs, grads = [m["recv"] for m in made], [g for m in made for g in m["all"]]
        every = sum(r.shape[0] for r in recvs)
        f_in = pl.BlockSpec((1, width, tile), lambda j, s: (0, 0, j))
        fishers.extend(
            run(
                functools.partial(fisher_body, 1.0 / rows, [len(m["all"]) for m in made]),
                [shape((1, width, hidden)), shape((1, width, hidden)), shape((1, hidden, width))],
                [side] + grads + recvs,
                "fisher",
                grid=(steps,),
                in_specs=[pl.BlockSpec((3, g.shape[1], tile), lambda j, s: (0, 0, j)) for g in grads]
                + [None] * len(recvs),
                out_specs=[f_in, f_in, pl.BlockSpec((1, tile, width), lambda j, s: (0, j, 0))],
                prefetch=1,
                scratch=[pltpu.VMEM((every, width), BF)] * 2,
            )
        )

    def total(last_one):
        parts = held + [p for m in made for p in m.pop("sums", [])]
        held[:] = run(total_body, [shape((rows, width), BF if last_one else F32)], parts, "total")

    fishers, held = [], []
    steps_of = {
        "pick": pick, "partial": partial, "pair": pair, "back": back, "input": input_grad, "combine": combine, "fisher": fisher, "total": total, "ring": ring,
    }
    for step, k in ORDER:
        steps_of[step](k)
    return (held[0], *fishers)


def solution(mesh):
    in_specs = (
        P("ep", "tp"),
        P("ep", "tp"),
        P("ep", None),
        P("ep", None),
        P("ep", "tp", None),
        P("ep", "tp", None),
        P("ep", None, "tp"),
    )
    out_specs = (P("ep", "tp"), P("ep", "tp", None), P("ep", "tp", None), P("ep", None, "tp"))
    return jax.shard_map(
        on_device, mesh=mesh, in_specs=in_specs, out_specs=out_specs, check_vma=False
    )
```

```python
import functools

import jax
import jax.numpy as jnp
from jax import lax
from jax.experimental import pallas as pl
from jax.experimental.pallas import tpu as pltpu
from jax.sharding import PartitionSpec as P

BF = jnp.bfloat16
F32 = jnp.float32
GROUP = 8
META = 16
COSTS = {'payload': 33210000, 'pick': 88560000, 'partial': 22140000, 'pair': 51660000, 'back': 62730000, 'input_grad': 221400000, 'combine': 46125000, 'fisher': 413280000, 'total': 73800000}
VMEM = 100 * 1024 * 1024 // 2
CHUNKS = ([0, -1, 1], [-2, 2], [-3, 3, 4])

ORDER = (
    ('ring', 2),
    ('ring', 3),
    ('ring', 4),
    ('pick', 0),
    ('pick', 1),
    ('partial', 0),
    ('partial', 1),
    ('pick', 2),
    ('pair', 0),
    ('pair', 1),
    ('back', 0),
    ('partial', 2),
    ('input', 0),
    ('back', 1),
    ('pair', 2),
    ('back', 2),
    ('combine', 0),
    ('input', 1),
    ('input', 2),
    ('combine', 1),
    ('combine', 2),
    ('fisher', 0),
    ('total', True),
)


def dot(left, right, dims):
    return lax.dot_general(left, right, ((dims[0], dims[1]), ((), ())), preferred_element_type=F32)


def call(body, outs, args, name, grid=(1,), in_specs=None, out_specs=None, prefetch=0, scratch=()):
    whole = lambda a: pl.BlockSpec(a.shape, lambda *_: (0,) * len(a.shape))
    ins = args[prefetch:]
    in_specs = [whole(a) if s is None else s for a, s in zip(ins, in_specs or [None] * len(ins))]
    out_specs = [whole(a) if s is None else s for a, s in zip(outs, out_specs or [None] * len(outs))]
    args = list(args[:prefetch]) + list(ins)
    return pl.pallas_call(
        body,
        out_shape=[pltpu.HBM(o.shape, o.dtype) for o in outs],
        grid_spec=pltpu.PrefetchScalarGridSpec(
            num_scalar_prefetch=prefetch,
            grid=grid,
            in_specs=in_specs,
            out_specs=out_specs,
            scratch_shapes=scratch,
        ),
        compiler_params=pltpu.CompilerParams(
            dimension_semantics=("arbitrary",) * len(grid), vmem_limit_bytes=VMEM
        ),
        cost_estimate=pl.CostEstimate(flops=COSTS[name] * 300, bytes_accessed=1, transcendentals=0),
        name=name,
    )(*args)


def payload_body(tok, grad, ids, probs, out):
    rows = tok.shape[0]
    out[0:rows, :] = tok[...]
    out[rows : 2 * rows, :] = grad[...]
    p = probs[...]
    high = p.astype(BF).astype(F32)
    mid = (p - high).astype(BF).astype(F32)
    low = p - high - mid
    pad = jnp.zeros((META - p.shape[0], p.shape[1]), F32)
    parts = [jnp.concatenate([v, pad], 0) for v in (ids[...].astype(F32), high, mid, low)]
    used = sum(v.shape[1] for v in parts)
    parts.append(jnp.zeros((META, out.shape[1] - used), F32))
    out[2 * rows :, :] = jnp.concatenate(parts, 1).astype(BF)


def pick_body(cap, place, *refs):
    pays, (send, pick) = refs[:-2], refs[-2:]
    count = len(pays)
    rows = (pays[0].shape[0] - META) // 2
    width = pays[0].shape[1]
    per = pick.shape[0] // GROUP
    first = place[0] // GROUP * GROUP
    before = (
        lax.broadcasted_iota(jnp.int32, (rows, rows), 0) < lax.broadcasted_iota(jnp.int32, (rows, rows), 1)
    ).astype(F32).astype(BF)
    expert = (lax.broadcasted_iota(jnp.int32, (GROUP, GROUP, rows), 0) + first).astype(F32)
    codes, probs = [], []
    for at, pay in enumerate(pays):
        meta = pay[2 * rows :, : 4 * rows].astype(F32)[:GROUP]
        ids, p = meta[:, :rows], meta[:, rows : 2 * rows] + meta[:, 2 * rows : 3 * rows] + meta[:, 3 * rows :]
        named = expert == ids[None]
        has = jnp.sum(jnp.where(named, 1.0, 0.0), 1)
        probs.append(jnp.sum(jnp.where(named, p[None], 0.0), 1))
        rank = dot(has.astype(BF), before, ((1,), (0,)))
        codes.append(jnp.where(has > 0.5, rank + 32.0 * at, -1.0))
    codes, probs = jnp.concatenate(codes, 1), jnp.concatenate(probs, 1)
    row = lax.broadcasted_iota(jnp.int32, (per, count * rows), 0)
    code = row
    for at in range(count):
        code = code + jnp.where(row >= cap * (at + 1), 32 - cap, 0)
    code = code.astype(F32)
    scales = []
    for d in range(GROUP):
        hit = code == codes[d : d + 1]
        pick[d * per : (d + 1) * per, :] = jnp.where(hit, 1.0, 0.0).astype(BF)
        scales.append(jnp.sum(jnp.where(hit, probs[d : d + 1], 0.0), 1, keepdims=True))
    onehot = pick[...]
    toks = jnp.concatenate([pay[0:rows, :] for pay in pays], 0)
    send[:, :width] = dot(onehot, toks, ((1,), (0,))).astype(BF)
    grads = jnp.concatenate([pay[rows : 2 * rows, :] for pay in pays], 0)
    send[:, width:] = (dot(onehot, grads, ((1,), (0,))) * jnp.concatenate(scales, 0)).astype(BF)


def partial_body(side, rows_ref, gate, up, down, send, keep, work):
    half = send.shape[1]
    width = gate.shape[1]
    kept = pl.multiple_of(side[0] * half, 16)
    sent = pl.multiple_of((1 - side[0]) * half, 16)
    for at in range(3):
        if at < 2:
            work[...] = dot(rows_ref[:, :width], (gate, up)[at][0], ((1,), (0,)))
        else:
            work[...] = dot(rows_ref[:, width:], down[0], ((1,), (1,)))
        send[at] = work[pl.ds(sent, half), :].astype(BF)
        keep[at] = work[pl.ds(kept, half), :].astype(BF)


def pair_body(side, keep, got, out):
    out[...] = (keep[...].astype(F32) + got[...].astype(F32)).astype(BF)


def swiglu_back(gate, up, dact):
    sig = 1.0 / (1.0 + jnp.exp(-gate))
    act = gate * sig * up
    dgate = dact * up * sig * (1.0 + gate * (1.0 - sig))
    return act.astype(BF), dgate.astype(BF), (dact * gate * sig).astype(BF)


def back_body(side, keep, got, more, out):
    sums = (keep[i].astype(F32) + got[i].astype(F32) + more[i].astype(F32) for i in range(3))
    out[0], out[1], out[2] = swiglu_back(*sums)


def places_of(side):
    h, q = side[0], side[1]
    return 2 * h + q, 2 * h + 1 - q, 2 * (1 - h) + q, 2 * (1 - h) + 1 - q


def input_body(side, own, near, far, last, gate, up, out, work):
    quarter = own.shape[1]

    @pl.when(pl.program_id(0) == 0)
    def _():
        for place, ref in zip(places_of(side), (own, near, far, last)):
            at = pl.ds(pl.multiple_of(place * quarter, 16), quarter)
            work[0, at, :] = ref[1]
            work[1, at, :] = ref[2]

    out[...] = (dot(work[0], gate[0], ((1,), (1,))) + dot(work[1], up[0], ((1,), (1,)))).astype(BF)


def square_bf(values):
    v = values.astype(F32)
    return (v * v).astype(BF)


def fisher_body(scale, cuts, side, *refs):
    grads, rows = refs[: sum(cuts)], refs[sum(cuts) : sum(cuts) + len(cuts)]
    f_gate, f_up, f_down, x_sq, dy_sq = refs[sum(cuts) + len(cuts) :]
    width = x_sq.shape[1]

    @pl.when(pl.program_id(0) == 0)
    def _():
        at = 0
        for ref, cut in zip(rows, cuts):
            part = ref.shape[0] // cut
            for place in places_of(side) if cut > 1 else (0,):
                values = ref[pl.ds(pl.multiple_of(place * part, 16), part), :]
                x_sq[at : at + part, :] = square_bf(values[:, :width])
                dy_sq[at : at + part, :] = square_bf(values[:, width:])
                at += part

    act, dgate, dup = (jnp.concatenate([square_bf(g[i]) for g in grads], 0) for i in range(3))
    f_gate[0] = (dot(x_sq[...], dgate, ((0,), (0,))) * scale).astype(BF)
    f_up[0] = (dot(x_sq[...], dup, ((0,), (0,))) * scale).astype(BF)
    f_down[0] = (dot(act, dy_sq[...], ((0,), (0,))) * scale).astype(BF)


def combine_body(pick, got, *outs):
    rows = outs[0].shape[0]
    for at, out in enumerate(outs):
        out[...] = dot(pick[:, at * rows : (at + 1) * rows], got[...], ((0,), (0,))).astype(out.dtype)


def total_body(*refs):
    total = refs[0][...].astype(F32)
    for ref in refs[1:-1]:
        total = total + ref[...].astype(F32)
    refs[-1][...] = total.astype(refs[-1].dtype)


def shape(dims, dtype=BF):
    return jax.ShapeDtypeStruct(dims, dtype)


def on_device(tokens, out_grad, expert_ids, route_probs, w_gate, w_up, w_down):
    rows, width = tokens.shape
    top = expert_ids.shape[1]
    ep, tp = lax.axis_size("ep"), lax.axis_size("tp")
    hidden = w_gate.shape[2]
    cap = rows * top * 9 // (8 * ep)
    deep = ep // GROUP
    groups = [[z * GROUP + i for i in range(GROUP)] for z in range(deep)]

    def along_z(value, step):
        n = ep * tp
        return lax.ppermute(value, ("ep", "tp"), [(i, (i + step * GROUP * tp) % n) for i in range(n)])

    def along_x(value, which):
        pairs = []
        for i in range(ep * tp):
            e, x = divmod(i, tp)
            pairs.append((i, e * tp + (x ^ 1 if (e % 2 == 0) == (which == 1) else 3 - x)))
        return lax.ppermute(value, ("ep", "tp"), pairs)

    def across(value):
        split = value.reshape(GROUP, -1, value.shape[1])
        return lax.all_to_all(
            split, "ep", split_axis=0, concat_axis=0, axis_index_groups=groups, tiled=True
        ).reshape(value.shape)

    e, x = lax.axis_index("ep"), lax.axis_index("tp")
    place = e.astype(jnp.int32).reshape(1)
    outer = (x ^ (x >> 1)) & 1
    upper = x >> 1
    even = e % 2 == 0
    side = jnp.stack([jnp.where(even, outer, upper), jnp.where(even, upper, outer)]).astype(jnp.int32)

    pays = {}
    (pays[0],) = call(
        payload_body,
        [shape((2 * rows + META, width))],
        [tokens, out_grad, expert_ids.T, route_probs.T],
        "payload",
    )
    pays[-1], pays[1] = along_z(pays[0], 1), along_z(pays[0], -1)

    tile = 256
    steps = hidden // tile
    last = [pays[0]]

    def run(body, outs, args, name, **kw):
        at = kw.get("prefetch", 0)
        args = list(args)
        args[at], _ = lax.optimization_barrier((args[at], last[0]))
        outs = call(body, outs, args, name, **kw)
        last[0] = outs[0]
        return outs

    made = [{} for _ in CHUNKS]

    def dims(k):
        count = len(CHUNKS[k])
        per = -(-count * cap // 8) * 8
        return count, GROUP * per, GROUP * per // 2, GROUP * per // 4

    def ring(step):
        for sign in (-1, 1):
            if step < deep // 2 or sign < 0:
                value, _ = lax.optimization_barrier((pays[sign * (step - 1)], last[0]))
                pays[sign * step if step < deep // 2 else step] = along_z(value, -sign)

    def pick(k):
        count, total, _, _ = dims(k)
        send, made[k]["pick"] = run(
            functools.partial(pick_body, cap),
            [shape((total, 2 * width)), shape((total, count * rows))],
            [place] + [pays[o] for o in CHUNKS[k]],
            "pick",
            prefetch=1,
        )
        made[k]["recv"] = across(send)

    def partial(k):
        _, total, half, _ = dims(k)
        w_in = pl.BlockSpec((1, width, tile), lambda j, s: (0, 0, j))
        half_out = pl.BlockSpec((3, half, tile), lambda j, s: (0, 0, j))
        give, made[k]["keep"] = run(
            partial_body,
            [shape((3, half, hidden))] * 2,
            [side, made[k]["recv"], w_gate, w_up, w_down],
            "partial",
            grid=(steps,),
            in_specs=[None, w_in, w_in, pl.BlockSpec((1, tile, width), lambda j, s: (0, j, 0))],
            out_specs=[half_out, half_out],
            prefetch=1,
            scratch=[pltpu.VMEM((total, tile), F32)],
        )
        made[k]["got"] = along_x(give, 1)

    def pair(k):
        quarter = dims(k)[3]
        theirs = pl.BlockSpec((3, quarter, hidden), lambda j, s: (0, 1 - s[1], 0))
        (give,) = run(
            pair_body,
            [shape((3, quarter, hidden))],
            [side, made[k]["keep"], made[k]["got"]],
            "pair",
            in_specs=[theirs, theirs],
            prefetch=1,
        )
        made[k]["more"] = along_x(give, 2)

    def back(k):
        quarter = dims(k)[3]
        mine = pl.BlockSpec((3, quarter, hidden), lambda j, s: (0, s[1], 0))
        (own,) = run(
            back_body,
            [shape((3, quarter, hidden))],
            [side, made[k]["keep"], made[k]["got"], made[k]["more"]],
            "back",
            in_specs=[mine, mine, None],
            prefetch=1,
        )
        near = along_x(own, 2)
        made[k]["all"] = [own, near, along_x(own, 1), along_x(near, 1)]

    def input_grad(k):
        _, total, _, _ = dims(k)
        w_out = pl.BlockSpec((1, tile, hidden), lambda j, s: (0, j, 0))
        (d_rows,) = run(
            input_body,
            [shape((total, width))],
            [side] + made[k]["all"] + [w_gate, w_up],
            "input_grad",
            grid=(width // tile,),
            in_specs=[None] * 4 + [w_out, w_out],
            out_specs=[pl.BlockSpec((total, tile), lambda j, s: (0, j))],
            prefetch=1,
            scratch=[pltpu.VMEM((2, total, hidden), BF)],
        )
        made[k]["back"] = across(d_rows)

    def combine(k):
        sums = run(
            combine_body,
            [shape((rows, width), BF if o else F32) for o in CHUNKS[k]],
            [made[k]["pick"], made[k]["back"]],
            "combine",
        )
        made[k]["sums"] = [along_z(s, o) if o else s for o, s in zip(CHUNKS[k], sums)]

    def fisher(_):
        recvs, grads = [m["recv"] for m in made], [g for m in made for g in m["all"]]
        every = sum(r.shape[0] for r in recvs)
        f_in = pl.BlockSpec((1, width, tile), lambda j, s: (0, 0, j))
        fishers.extend(
            run(
                functools.partial(fisher_body, 1.0 / rows, [len(m["all"]) for m in made]),
                [shape((1, width, hidden)), shape((1, width, hidden)), shape((1, hidden, width))],
                [side] + grads + recvs,
                "fisher",
                grid=(steps,),
                in_specs=[pl.BlockSpec((3, g.shape[1], tile), lambda j, s: (0, 0, j)) for g in grads]
                + [None] * len(recvs),
                out_specs=[f_in, f_in, pl.BlockSpec((1, tile, width), lambda j, s: (0, j, 0))],
                prefetch=1,
                scratch=[pltpu.VMEM((every, width), BF)] * 2,
            )
        )

    def total(last_one):
        parts = held + [p for m in made for p in m.pop("sums", [])]
        held[:] = run(total_body, [shape((rows, width), BF if last_one else F32)], parts, "total")

    fishers, held = [], []
    steps_of = {
        "pick": pick, "partial": partial, "pair": pair, "back": back, "input": input_grad, "combine": combine, "fisher": fisher, "total": total, "ring": ring,
    }
    for step, k in ORDER:
        steps_of[step](k)
    return (held[0], *fishers)


def solution(mesh):
    in_specs = (
        P("ep", "tp"),
        P("ep", "tp"),
        P("ep", None),
        P("ep", None),
        P("ep", "tp", None),
        P("ep", "tp", None),
        P("ep", None, "tp"),
    )
    out_specs = (P("ep", "tp"), P("ep", "tp", None), P("ep", "tp", None), P("ep", None, "tp"))
    return jax.shard_map(
        on_device, mesh=mesh, in_specs=in_specs, out_specs=out_specs, check_vma=False
    )
```
